32 devices in a mesh: gx: 4 (over y, x), gy: 8 (over z, core).
Axes of the slice: x: 2, y: 2, z: 4, core: 2. Of those that a mesh axis runs over, the one named last changes fastest.
Arguments:
- traveltime: float32 [8, 32, 64, 512], P(None, None, 'gy', 'gx'), may hold values from 1 to 4
- adjoint_start: float32 [8, 32, 64, 512], P(None, None, 'gy', 'gx'), may hold values from -6 to 6
- upwind_flags: int32 [8, 32, 64, 512], P(None, None, 'gy', 'gx'), may hold values from 0 to 7, as said below
- slowness: float32 [32, 64, 512], P(None, 'gy', 'gx'), may hold values from 0.15 to 0.6
- residual_rows: float32 [2048, 8], P(('gx', 'gy')), may hold values from -6 to 6
- station_tile: int32 [2048, 1], P(('gx', 'gy')), may hold values from 0 to 31; in each aligned block of 64 rows (0 to 63, 64 to 127, ...) at most 4 rows name the same one
- station_cell: int32 [2048], P(('gx', 'gy')), may hold values from 0 to 32767
Outputs:
- adjoint: float32 [8, 32, 64, 512], P(None, None, 'gy', 'gx')
- gradient: float32 [32, 64, 512], P(None, 'gy', 'gx')
The draws below stay inside these ranges and needn't reach their ends.
Inputs may be any that keep to these rules, and one draw needn't show every extreme that they name: `upwind_flags`: bit k of a cell's value is 1 where its upwind neighbour along x, y, z (k = 0, 1, 2) lies at the higher index; at every face of the grid the upwind neighbour lies inside the grid. `station_tile`: among the records of one device no tile is named more than 4 times, a bound that some block reaches.
All inputs are finite; a program needn't handle non-finite values.
Results may differ from the reference program's by a relative error of at most 0.00002.
Values sent between devices are 32-bit elements; how exact they have to be, the bound alone decides.
A program may use at most 128 MiB of HBM per device.

```python
import math
import jax
import jax.numpy as jnp
import numpy as np
from jax import lax

S = 8
Z = 32
TY = 8
TX = 128
SWEEPS = 3
CAP = 4
ST_DEV = 64
STATIONS = 2048
NX = 512
NY = 64
N_GY = 8
DEVICES = 32


def draw_upwind_flags(key, part):
    shape = (S, Z, NY, NX)
    bits = jax.random.randint(key, shape, 0, 8)
    along_x = bits % 2
    along_y = bits // 2 % 2
    along_z = bits // 4
    place_x = lax.broadcasted_iota(jnp.int32, shape, 3)
    place_y = lax.broadcasted_iota(jnp.int32, shape, 2)
    place_z = lax.broadcasted_iota(jnp.int32, shape, 1)
    along_x = jnp.where(place_x == 0, 1, jnp.where(place_x == NX - 1, 0, along_x))
    along_y = jnp.where(place_y == 0, 1, jnp.where(place_y == NY - 1, 0, along_y))
    along_z = jnp.where(place_z == 0, 1, jnp.where(place_z == Z - 1, 0, along_z))
    return (along_x + 2 * along_y + 4 * along_z).astype(jnp.int32)


def with_ends(result, own_key, low, top_value):
    spot = [jax.random.randint(jax.random.fold_in(own_key, axis), (), 0, length) for axis, length in enumerate(result.shape)]
    main_axis = result.shape.index(max(result.shape))
    neighbour = spot[:main_axis] + [(spot[main_axis] + 1) % result.shape[main_axis]] + spot[main_axis + 1:]
    return result.at[tuple(spot)].set(low).at[tuple(neighbour)].set(top_value)


def steps_of(own_key, extent, pieces, least, top_value):
    def one(axis_at, blocks):
        steps = jax.random.uniform(jax.random.fold_in(jax.random.fold_in(own_key, 6), axis_at), (blocks,), jnp.float32, least / len(pieces), top_value / len(pieces))
        return jnp.repeat(jnp.exp(steps), extent[axis_at] // blocks).reshape((-1,) + (1,) * (len(extent) - axis_at - 1))

    loudness = one(*pieces[0])
    for cut in pieces[1:]:
        loudness = loudness * one(*cut)
    return loudness


def shared_out(own_key, own, number, rows, amount, top, most, slope):
    order = jax.random.permutation(own_key, amount)
    crowded, usual = shares(amount, rows * top, most, slope, True), shares(amount, rows * top, most, slope, False)
    places = jnp.arange(amount)

    def named(sizes, turn):
        used = int((sizes > 0).sum())
        fixed = max(1, used // 4)
        moved = fixed + (places - fixed + turn * (used - fixed)) % max(1, amount - fixed)
        return jnp.zeros((amount,), jnp.int32).at[order[jnp.where(places < fixed, places, moved)]].set(jnp.asarray(sizes, jnp.int32))

    sizes = jnp.where(number % 4 == 0, named(crowded, number // 4), named(usual, number - number // 4 - 1))
    mixed = jax.random.permutation(jax.random.fold_in(own, 3), amount)
    donor, taker = mixed[0:amount // 2 * 2:2], mixed[1:amount // 2 * 2:2]
    slack = jnp.minimum(sizes[donor] - 1, most - sizes[taker]) // 2
    slack = jnp.where((donor == order[0]) | (taker == order[0]) | (sizes[taker] == 0), 0, jnp.maximum(slack, 0))
    moved = jax.random.randint(jax.random.fold_in(own, 4), (amount // 2,), 0, 1 << 20) % (slack + 1)
    sizes = sizes.at[donor].add(-moved).at[taker].add(moved)
    members = jnp.searchsorted(jnp.cumsum(sizes), jnp.arange(rows * top), side="right").astype(jnp.int32)
    grid = members.reshape(top, rows).T
    grid = grid[jax.random.permutation(jax.random.fold_in(own, 1), rows)]
    turn = jax.random.randint(jax.random.fold_in(own, 2), (rows, 1), 0, top)
    return jnp.take_along_axis(grid, (jnp.arange(top)[None, :] + turn) % top, axis=1)


def shares(count, total, most, skew, full):
    portions = [(1 << 20) // math.isqrt(rank ** skew) + 1 for rank in range(1, count + 1)]
    largest = most if full else min(most, max(-(-total // count), total * portions[0] // sum(portions)))
    least = 1 if total - largest >= count - 1 else 0
    given, surplus = [largest] + [least] * (count - 1), total - largest - least * (count - 1)
    while surplus > 0:
        movable = [i for i in range(1, count) if given[i] < largest] or [i for i in range(1, count) if given[i] < most]
        pool, budget = sum([portions[i] for i in movable]), surplus
        for i in movable:
            more = min(most - given[i], max(1, budget * portions[i] // pool), surplus)
            given[i] = given[i] + more
            surplus = surplus - more
    return np.array(given)


def normal_values(own_key, dims, width, most, pieces=(), kind=jnp.bfloat16):
    drawn = width * jax.random.normal(own_key, dims, jnp.float32)
    if pieces:
        drawn = drawn * steps_of(own_key, dims, pieces, -0.22, 0.18)
    return jnp.clip(drawn, -most, most).astype(kind)


def setup_inputs(seed: int = 0) -> dict:
    key_of = jax.random.split(jax.random.key(seed), 8)
    traveltime = jnp.clip(1.0 + 3.0 * jax.random.uniform(key_of[0], (S, Z, NY, NX), jnp.float32) ** steps_of(key_of[0], (S, Z, NY, NX), ((2, 8), (3, 4)), -0.2, 0.2), 1.0, 4.0)
    adjoint_start = normal_values(key_of[1], (S, Z, NY, NX), 1.0, 6.0, ((2, 8), (3, 4)), jnp.float32)
    upwind_flags = draw_upwind_flags(jax.random.fold_in(key_of[7], 71), 0)
    slowness = jnp.clip(jnp.exp(math.log(0.6) - 1.3862944 * jax.random.uniform(key_of[3], (Z, NY, NX), jnp.float32) ** steps_of(key_of[3], (Z, NY, NX), ((1, 8), (2, 4)), -0.2, 0.2)), 0.15, 0.6)
    residual_rows = normal_values(key_of[4], (STATIONS, S), 1.0, 6.0, ((0, 32),), jnp.float32)
    station_tile_keys = jax.random.split(jax.random.fold_in(key_of[5], 1), STATIONS // ST_DEV)
    station_tile_turns = jax.random.permutation(jax.random.fold_in(key_of[5], 3), STATIONS // ST_DEV)
    station_tile = jax.vmap(lambda own, number: shared_out(jax.random.fold_in(key_of[5], 2), own, number, ST_DEV, DEVICES, 1, CAP, 1))(station_tile_keys, station_tile_turns).reshape((STATIONS, 1))
    station_cell = with_ends(jax.random.randint(key_of[6], (STATIONS,), 0, Z * TY * TX), jax.random.fold_in(key_of[6], 1), 0, (Z * TY * TX) - 1).astype(jnp.int32)
    return {"traveltime": traveltime, "adjoint_start": adjoint_start, "upwind_flags": upwind_flags, "slowness": slowness, "residual_rows": residual_rows, "station_tile": station_tile, "station_cell": station_cell}


def hpad(values):
    widths = [(0, 0)] * (values.ndim - 2) + [(1, 1), (1, 1)]
    return jnp.pad(values, widths)


def relax(adjoint, push_x, push_y, push_z, source, denominator):
    plus_x = jnp.maximum(push_x, 0.0) * adjoint
    minus_x = jnp.maximum(-push_x, 0.0) * adjoint
    plus_y = jnp.maximum(push_y, 0.0) * adjoint
    minus_y = jnp.maximum(-push_y, 0.0) * adjoint
    plus_z = jnp.pad(jnp.maximum(push_z, 0.0) * adjoint, ((0, 0), (1, 1), (0, 0), (0, 0)))
    minus_z = jnp.pad(jnp.maximum(-push_z, 0.0) * adjoint, ((0, 0), (1, 1), (0, 0), (0, 0)))
    inflow = plus_x[:, :, 1:-1, :-2] + minus_x[:, :, 1:-1, 2:] + plus_y[:, :, :-2, 1:-1] + minus_y[:, :, 2:, 1:-1]
    vertical = plus_z[:, :-2] + minus_z[:, 2:]
    inflow = inflow + vertical[:, :, 1:-1, 1:-1]
    return (source[:, :, 1:-1, 1:-1] + inflow) / denominator[:, :, 1:-1, 1:-1]


def smooth(extended):
    centre = extended[:, 1:-1, 1:-1]
    beside = extended[:, 1:-1, 2:] + extended[:, 1:-1, :-2] + extended[:, 2:, 1:-1] + extended[:, :-2, 1:-1]
    return centre + 0.125 * (beside - 4.0 * centre)


def reference(traveltime, adjoint_start, upwind_flags, slowness, residual_rows, station_tile, station_cell):
    sources, levels, rows_y, rows_x = traveltime.shape
    tiles = station_tile[:, 0]
    tile_x = tiles // N_GY
    tile_y = tiles % N_GY
    level = station_cell // (TY * TX)
    cell_y = tile_y * TY + (station_cell // TX) % TY
    cell_x = tile_x * TX + station_cell % TX
    flat = ((level * rows_y + cell_y) * rows_x + cell_x).astype(jnp.int32)
    source = jnp.zeros((sources, levels * rows_y * rows_x), jnp.float32)
    source = source.at[:, flat].add(residual_rows.T).reshape(sources, levels, rows_y, rows_x)
    padded = jnp.pad(traveltime, ((0, 0), (1, 1), (1, 1), (1, 1)))
    plus_x = (upwind_flags % 2) == 1
    plus_y = ((upwind_flags // 2) % 2) == 1
    plus_z = (upwind_flags // 4) == 1
    up_x = jnp.where(plus_x, padded[:, 1:-1, 1:-1, 2:], padded[:, 1:-1, 1:-1, :-2])
    up_y = jnp.where(plus_y, padded[:, 1:-1, 2:, 1:-1], padded[:, 1:-1, :-2, 1:-1])
    up_z = jnp.where(plus_z, padded[:, 2:, 1:-1, 1:-1], padded[:, :-2, 1:-1, 1:-1])
    coef_x = jnp.maximum(traveltime - up_x, 0.0)
    coef_y = jnp.maximum(traveltime - up_y, 0.0)
    coef_z = jnp.maximum(traveltime - up_z, 0.0)
    push_x = jnp.where(plus_x, coef_x, -coef_x)
    push_y = jnp.where(plus_y, coef_y, -coef_y)
    push_z = jnp.where(plus_z, coef_z, -coef_z)
    denominator = 1.0 + coef_x + coef_y + coef_z
    adjoint = adjoint_start
    for repeat in range(SWEEPS):
        adjoint = relax(hpad(adjoint), hpad(push_x), hpad(push_y), hpad(push_z), hpad(source), hpad(denominator))
    total = jnp.sum(adjoint, axis=0)
    gradient = slowness * smooth(hpad(total))
    return adjoint, gradient
```

```python
import functools

import jax
import jax.numpy as jnp
from jax import lax
from jax.experimental import pallas as pl
from jax.experimental.pallas import tpu as pltpu
from jax.sharding import PartitionSpec as P

SWEEPS = 3
CAP = 4
MESH = pl.DeviceIdType.MESH
F32 = jnp.float32
BF16 = jnp.bfloat16
FIELDS = 32


def roll(x, shift, axis):
    return pltpu.roll(x, shift % x.shape[axis], axis)


def kernel(
    n_gx, n_gy,
    t_h, a_h, f_h, slow_h, rows_h, tile_h, cell_h,
    adj_h, grad_h,
    tv, fv, a0, a1, slv, rowsv, tilev, cellv, gradv,
    c_l, c_r, c_u, c_d, c_b, c_t, sp, total,
    rec, msg, box,
    ey_hi, ey_lo, ex, ry_hi, ry_lo, rx,
    oy_hi, oy_lo, ox, iy_lo, iy_hi, ix_lo, ix_hi,
    toy_hi, toy_lo, tox, tiy_lo, tiy_hi, tix_lo, tix_hi,
    in_sem, small_sem, send_sem, recv_sem, tsend, trecv, st_send, st_recv, out_sem,
):
    sources, levels, rows_n, lanes_n = tv.shape
    devices = n_gx * n_gy
    mx = lax.axis_index("gx")
    my = lax.axis_index("gy")
    me = mx * n_gy + my

    barrier = pltpu.get_barrier_semaphore()
    others = [(dx, dy) for dx in range(n_gx) for dy in range(n_gy) if dx or dy]

    def far(dx, dy):
        return lax.rem(mx + dx, n_gx), lax.rem(my + dy, n_gy)

    for dx, dy in others:
        pl.semaphore_signal(barrier, inc=1, device_id=far(dx, dy), device_id_type=MESH)

    small = [
        pltpu.make_async_copy(src, dst, small_sem.at[k])
        for k, (src, dst) in enumerate(
            [(tile_h, tilev), (rows_h, rowsv), (cell_h, cellv), (slow_h, slv)]
        )
    ]
    for copy in small:
        copy.start()

    def load(k, src, dst, s):
        return pltpu.make_async_copy(src.at[s], dst.at[s], in_sem.at[k, s])

    for k, (src, dst) in enumerate([(t_h, tv), (a_h, a0), (f_h, fv)]):
        for s in range(sources):
            load(k, src, dst, s).start()

    sub = lax.broadcasted_iota(jnp.int32, (rows_n, lanes_n), 0)
    lane = lax.broadcasted_iota(jnp.int32, (rows_n, lanes_n), 1)
    first_row, last_row = sub == 0, sub == rows_n - 1
    first_lane, last_lane = lane == 0, lane == lanes_n - 1
    odd = lane % 2 == 1

    @pl.when(my == 0)
    def _():
        iy_lo[...] = jnp.zeros_like(iy_lo)
        tiy_lo[...] = jnp.zeros_like(tiy_lo)

    @pl.when(my == n_gy - 1)
    def _():
        iy_hi[...] = jnp.zeros_like(iy_hi)
        tiy_hi[...] = jnp.zeros_like(tiy_hi)

    @pl.when(mx == 0)
    def _():
        ix_lo[...] = jnp.zeros_like(ix_lo)
        tix_lo[...] = jnp.zeros_like(tix_lo)

    @pl.when(mx == n_gx - 1)
    def _():
        ix_hi[...] = jnp.zeros_like(ix_hi)
        tix_hi[...] = jnp.zeros_like(tix_hi)

    for copy in small[:3]:
        copy.wait()
    count = rowsv.shape[0]
    r_i = lax.broadcasted_iota(jnp.int32, (count, count), 0)
    c_i = lax.broadcasted_iota(jnp.int32, (count, count), 1)
    eye = r_i == c_i
    tile_row = jnp.sum(jnp.where(eye, tilev[...].astype(F32), 0.0), axis=0, keepdims=True)
    cell_col = jnp.sum(jnp.where(eye, cellv[...].astype(F32), 0.0), axis=1, keepdims=True)
    cell_row_f = jnp.floor(cell_col * (1.0 / lanes_n))
    rec[...] = jnp.zeros_like(rec)
    rec[:, 0:sources] = rowsv[...]
    rec[:, sources : sources + 1] = cell_row_f
    rec[:, sources + 1 : sources + 2] = cell_col - cell_row_f * lanes_n
    d_i = lax.broadcasted_iota(jnp.int32, (devices, count), 0).astype(F32)
    named = jnp.where(d_i == tile_row, 1.0, 0.0)
    earlier = jnp.where(r_i < c_i, 1.0, 0.0)
    rank = jnp.dot(named.astype(BF16), earlier.astype(BF16), preferred_element_type=F32)
    base = rec[...]
    b_hi = base.astype(BF16)
    left = base - b_hi.astype(F32)
    b_mid = left.astype(BF16)
    b_lo = (left - b_mid.astype(F32)).astype(BF16)
    slots = jnp.zeros((devices, lanes_n), F32)
    for c in range(CAP):
        pick = jnp.where((named > 0.0) & (rank == float(c)), 1.0, 0.0).astype(BF16)
        got = (
            jnp.dot(pick, b_lo, preferred_element_type=F32)
            + jnp.dot(pick, b_mid, preferred_element_type=F32)
            + jnp.dot(pick, b_hi, preferred_element_type=F32)
        )
        slots = slots + (roll(got, FIELDS * c, 1) if c else got)
    for d in range(devices):
        msg[d] = slots[d : d + 1, :]

    def packed(acc, plane, z):
        return jnp.where((lane == 2 * z) | (lane == 2 * z + 1), roll(plane, 2 * z + 1, 1), acc)

    def edges_of(s, _):
        load(0, t_h, tv, s).wait()
        load(1, a_h, a0, s).wait()
        acc_t = jnp.zeros((rows_n, lanes_n), F32)
        acc_a = jnp.zeros((rows_n, lanes_n), F32)
        for z in range(levels):
            t = tv[s, z]
            a = a0[s, z]
            oy_hi[0, s, z : z + 1, :] = t[rows_n - 1 : rows_n]
            oy_lo[0, s, z : z + 1, :] = t[0:1]
            ry_hi[s, z : z + 1, :] = a[rows_n - 1 : rows_n]
            ry_lo[s, z : z + 1, :] = a[0:1]
            acc_t = packed(acc_t, t, z)
            acc_a = packed(acc_a, a, z)
        ox[0, s] = acc_t
        rx[s] = acc_a
        return 0

    lax.fori_loop(0, sources, edges_of, 0)

    pl.semaphore_wait(barrier, devices - 1)

    def halo(k, s):
        def one(way, src, dst, dev):
            return pltpu.make_async_remote_copy(
                src_ref=src.at[k, s], dst_ref=dst.at[k, s],
                send_sem=send_sem.at[k, way, s], recv_sem=recv_sem.at[k, way, s],
                device_id=dev, device_id_type=MESH,
            )
        up = (mx, lax.rem(my + 1, n_gy))
        down = (mx, lax.rem(my + n_gy - 1, n_gy))
        right = (lax.rem(mx + 1, n_gx), my)
        left_ = (lax.rem(mx + n_gx - 1, n_gx), my)
        return (
            (one(0, oy_hi, iy_lo, up), my < n_gy - 1, my > 0),
            (one(1, oy_lo, iy_hi, down), my > 0, my < n_gy - 1),
            (one(2, ox, ix_lo, right), mx < n_gx - 1, mx > 0),
            (one(3, ox, ix_hi, left_), mx > 0, mx < n_gx - 1),
        )

    def send(k, s):
        for copy, sends, _ in halo(k, s):
            @pl.when(sends)
            def _(copy=copy):
                copy.start()

    def arrive(k, s):
        for copy, _, takes in halo(k, s):
            @pl.when(takes)
            def _(copy=copy):
                copy.wait_recv()

    def send_all(s, _):
        send(0, s)
        return 0

    lax.fori_loop(0, sources, send_all, 0)

    own = pltpu.make_async_copy(msg.at[me], box.at[me], st_recv)
    for dx, dy in others:
        ox_, oy_ = far(dx, dy)
        pltpu.make_async_remote_copy(
            src_ref=msg.at[ox_ * n_gy + oy_], dst_ref=box.at[me],
            send_sem=st_send, recv_sem=st_recv,
            device_id=(ox_, oy_), device_id_type=MESH,
        ).start()
    own.start()

    def coefficients(s, _):
        load(2, f_h, fv, s).wait()
        arrive(0, s)
        acc = jnp.zeros((rows_n, lanes_n), F32)
        comb = jnp.where(odd, ix_hi[0, s], ix_lo[0, s])
        below = jnp.zeros((rows_n, lanes_n), F32)
        z_plus_before = jnp.zeros((rows_n, lanes_n), F32)
        r_before = None
        t = tv[s, 0]
        for z in range(levels):
            above = tv[s, z + 1] if z + 1 < levels else jnp.zeros((rows_n, lanes_n), F32)
            flags = fv[s, z]
            is_x, is_y, is_z = (flags & 1) == 1, (flags & 2) == 2, (flags & 4) == 4
            u = roll(comb, -(2 * z + 1), 1)
            t_l = roll(jnp.where(last_lane, u, t), 1, 1)
            t_r = roll(jnp.where(first_lane, u, t), -1, 1)
            t_u = jnp.where(first_row, iy_lo[0, s, z : z + 1, :], roll(t, 1, 0))
            t_d = jnp.where(last_row, iy_hi[0, s, z : z + 1, :], roll(t, -1, 0))
            k_x = jnp.maximum(t - jnp.where(is_x, t_r, t_l), 0.0)
            k_y = jnp.maximum(t - jnp.where(is_y, t_d, t_u), 0.0)
            k_z = jnp.maximum(t - jnp.where(is_z, above, below), 0.0)
            r = 1.0 / (1.0 + k_x + k_y + k_z)
            x_plus, x_minus = jnp.where(is_x, k_x, 0.0), jnp.where(is_x, 0.0, k_x)
            y_plus, y_minus = jnp.where(is_y, k_y, 0.0), jnp.where(is_y, 0.0, k_y)
            z_plus, z_minus = jnp.where(is_z, k_z, 0.0), jnp.where(is_z, 0.0, k_z)
            c_l[s, z] = roll(jnp.where(last_lane, 1.0, x_plus), 1, 1) * r
            c_r[s, z] = roll(jnp.where(first_lane, 1.0, x_minus), -1, 1) * r
            c_u[s, z] = roll(jnp.where(last_row, 1.0, y_plus), 1, 0) * r
            c_d[s, z] = roll(jnp.where(first_row, 1.0, y_minus), -1, 0) * r
            c_b[s, z] = z_plus_before * r
            if z:
                c_t[s, z - 1] = z_minus * r_before
            sp[s, z] = r
            ey_hi[s, z : z + 1, :] = y_plus[rows_n - 1 : rows_n]
            ey_lo[s, z : z + 1, :] = y_minus[0:1]
            acc = packed(acc, jnp.where(first_lane, x_minus, x_plus), z)
            below, t = t, above
            z_plus_before, r_before = z_plus, r
        c_t[s, levels - 1] = jnp.zeros((rows_n, lanes_n), F32)
        ex[s] = acc
        oy_hi[1, s] = ey_hi[s] * ry_hi[s]
        oy_lo[1, s] = ey_lo[s] * ry_lo[s]
        ox[1, s] = acc * rx[s]
        send(1, s)
        return 0

    lax.fori_loop(0, sources, coefficients, 0)

    pltpu.make_async_copy(box, box, st_recv).wait()
    boxes = jnp.concatenate([box[d] for d in range(devices)], axis=0)
    stacked = jnp.concatenate(
        [boxes] + [roll(boxes, -FIELDS * c, 1) for c in range(1, CAP)], axis=0
    )
    fields = stacked.T
    amount = stacked.shape[0]
    values = fields[0:sources]
    v_hi = values.astype(BF16).astype(F32)
    v_left = values - v_hi
    v_mid = v_left.astype(BF16).astype(F32)
    v_lo = v_left - v_mid
    at_row = fields[sources : sources + 1]
    at_lane = fields[sources + 1 : sources + 2]
    row_i = lax.broadcasted_iota(jnp.int32, (levels * rows_n, amount), 0).astype(F32)
    lane_i = lax.broadcasted_iota(jnp.int32, (lanes_n, amount), 0).astype(F32)
    in_row = jnp.where(row_i == at_row, 1.0, 0.0).astype(BF16)
    in_lane = lane_i == at_lane
    for s in range(sources):
        spread = None
        for part in (v_lo, v_mid, v_hi):
            weights = jnp.where(in_lane, part[s : s + 1], 0.0).astype(BF16)
            term = lax.dot_general(
                in_row, weights, (((1,), (1,)), ((), ())), preferred_element_type=F32
            )
            spread = term if spread is None else spread + term
        sp[s] = sp[s] * spread.reshape(levels, rows_n, lanes_n)

    total[...] = jnp.zeros_like(total)

    def sweep(k, src, dst, s):
        last = k == SWEEPS
        arrive(k, s)
        acc = jnp.zeros((rows_n, lanes_n), F32)
        comb = jnp.where(odd, ix_hi[k, s], ix_lo[k, s])
        below = None
        a = src[s, 0]
        for z in range(levels):
            above = src[s, z + 1] if z + 1 < levels else None
            u = roll(comb, -(2 * z + 1), 1)
            a_l = roll(jnp.where(last_lane, u, a), 1, 1)
            a_r = roll(jnp.where(first_lane, u, a), -1, 1)
            a_u = jnp.where(first_row, iy_lo[k, s, z : z + 1, :], roll(a, 1, 0))
            a_d = jnp.where(last_row, iy_hi[k, s, z : z + 1, :], roll(a, -1, 0))
            out = (sp[s, z] + c_l[s, z] * a_l) + (c_r[s, z] * a_r + c_u[s, z] * a_u)
            out = out + c_d[s, z] * a_d
            if below is not None:
                out = out + c_b[s, z] * below
            if above is not None:
                out = out + c_t[s, z] * above
            dst[s, z] = out
            if last:
                total[z] = total[z] + out
            else:
                ry_hi[s, z : z + 1, :] = out[rows_n - 1 : rows_n]
                ry_lo[s, z : z + 1, :] = out[0:1]
                acc = packed(acc, out, z)
            below, a = a, above
        if last:
            pltpu.make_async_copy(dst.at[s], adj_h.at[s], out_sem.at[s]).start()
        else:
            oy_hi[k + 1, s] = ey_hi[s] * ry_hi[s]
            oy_lo[k + 1, s] = ey_lo[s] * ry_lo[s]
            ox[k + 1, s] = ex[s] * acc
            send(k + 1, s)
        return 0

    held = (a0, a1)
    for k in range(1, SWEEPS + 1):
        src, dst = held[(k - 1) % 2], held[k % 2]
        lax.fori_loop(0, sources, lambda s, _, k=k, src=src, dst=dst: sweep(k, src, dst, s), 0)
    result = held[SWEEPS % 2]

    acc = jnp.zeros((rows_n, lanes_n), F32)
    for z in range(levels):
        cells = total[z]
        toy_hi[z : z + 1, :] = cells[rows_n - 1 : rows_n]
        toy_lo[z : z + 1, :] = cells[0:1]
        acc = packed(acc, cells, z)
    tox[...] = acc

    def last_copy(way, src, dst, dev):
        return pltpu.make_async_remote_copy(
            src_ref=src, dst_ref=dst, send_sem=tsend.at[way], recv_sem=trecv.at[way],
            device_id=dev, device_id_type=MESH,
        )

    finals = (
        (last_copy(0, toy_hi, tiy_lo, (mx, lax.rem(my + 1, n_gy))), my < n_gy - 1, my > 0),
        (last_copy(1, toy_lo, tiy_hi, (mx, lax.rem(my + n_gy - 1, n_gy))), my > 0, my < n_gy - 1),
        (last_copy(2, tox, tix_lo, (lax.rem(mx + 1, n_gx), my)), mx < n_gx - 1, mx > 0),
        (last_copy(3, tox, tix_hi, (lax.rem(mx + n_gx - 1, n_gx), my)), mx > 0, mx < n_gx - 1),
    )
    for copy, sends, _ in finals:
        @pl.when(sends)
        def _(copy=copy):
            copy.start()

    def drained(s, _):
        for k in range(SWEEPS + 1):
            for copy, sends, _ in halo(k, s):
                @pl.when(sends)
                def _(copy=copy):
                    copy.wait_send()
        return 0

    lax.fori_loop(0, sources, drained, 0)
    rest = msg.at[pl.ds(0, devices - 1)]
    pltpu.make_async_copy(rest, rest, st_send).wait()
    small[3].wait()

    for copy, _, takes in finals:
        @pl.when(takes)
        def _(copy=copy):
            copy.wait_recv()

    comb = jnp.where(odd, tix_hi[...], tix_lo[...])
    for z in range(levels):
        cells = total[z]
        u = roll(comb, -(2 * z + 1), 1)
        beside = (
            roll(jnp.where(last_lane, u, cells), 1, 1)
            + roll(jnp.where(first_lane, u, cells), -1, 1)
        ) + (
            jnp.where(first_row, tiy_lo[z : z + 1, :], roll(cells, 1, 0))
            + jnp.where(last_row, tiy_hi[z : z + 1, :], roll(cells, -1, 0))
        )
        gradv[z] = slv[z] * (cells + 0.125 * (beside - 4.0 * cells))
    out_grad = pltpu.make_async_copy(gradv, grad_h, out_sem.at[sources])
    out_grad.start()
    for copy, sends, _ in finals:
        @pl.when(sends)
        def _(copy=copy):
            copy.wait_send()
    for s in range(sources):
        pltpu.make_async_copy(result.at[s], adj_h.at[s], out_sem.at[s]).wait()
    out_grad.wait()


def shards(
    n_gx, n_gy,
    traveltime, adjoint_start, upwind_flags, slowness, residual_rows, station_tile, station_cell,
):
    sources, levels, rows_n, lanes_n = traveltime.shape
    devices = n_gx * n_gy
    rounds = SWEEPS + 1
    big = pltpu.VMEM(traveltime.shape, F32)
    flat = pltpu.VMEM(slowness.shape, F32)
    yrows = pltpu.VMEM((sources, levels, lanes_n), F32)
    xcols = pltpu.VMEM((sources, rows_n, lanes_n), F32)
    ymsg = pltpu.VMEM((rounds, sources, levels, lanes_n), F32)
    xmsg = pltpu.VMEM((rounds, sources, rows_n, lanes_n), F32)
    ytot = pltpu.VMEM((levels, lanes_n), F32)
    xtot = pltpu.VMEM((rows_n, lanes_n), F32)
    count = residual_rows.shape[0]
    dma = pltpu.SemaphoreType.DMA
    return pl.pallas_call(
        functools.partial(kernel, n_gx, n_gy),
        out_shape=(
            jax.ShapeDtypeStruct(traveltime.shape, F32),
            jax.ShapeDtypeStruct(slowness.shape, F32),
        ),
        in_specs=[pl.BlockSpec(memory_space=pl.ANY)] * 7,
        out_specs=[pl.BlockSpec(memory_space=pl.ANY)] * 2,
        scratch_shapes=[
            big, pltpu.VMEM(traveltime.shape, jnp.int32), big, big, flat,
            pltpu.VMEM(residual_rows.shape, F32),
            pltpu.VMEM(station_tile.shape, jnp.int32),
            pltpu.VMEM((1, count), jnp.int32),
            flat,
            big, big, big, big, big, big, big, flat,
            pltpu.VMEM((count, lanes_n), F32),
            pltpu.VMEM((devices, 1, lanes_n), F32),
            pltpu.VMEM((devices, 1, lanes_n), F32),
            yrows, yrows, xcols, yrows, yrows, xcols,
            ymsg, ymsg, xmsg, ymsg, ymsg, xmsg, xmsg,
            ytot, ytot, xtot, ytot, ytot, xtot, xtot,
            dma((3, sources)), dma((4,)),
            dma((rounds, 4, sources)), dma((rounds, 4, sources)),
            dma((4,)), dma((4,)), dma, dma, dma((sources + 1,)),
        ],
        compiler_params=pltpu.CompilerParams(
            collective_id=0, has_side_effects=True, vmem_limit_bytes=32 * 1024 * 1024
        ),
        name="tomography",
    )(
        traveltime, adjoint_start, upwind_flags, slowness, residual_rows, station_tile,
        station_cell.reshape(1, count),
    )


def solution(mesh):
    wide = P(None, None, "gy", "gx")
    placed = (
        wide, wide, wide, P(None, "gy", "gx"),
        P(("gx", "gy"), None), P(("gx", "gy"), None), P(("gx", "gy")),
    )
    return jax.shard_map(
        functools.partial(shards, mesh.shape["gx"], mesh.shape["gy"]),
        mesh=mesh,
        in_specs=placed,
        out_specs=(wide, P(None, "gy", "gx")),
        check_vma=False,
    )
```

```python
import functools

import jax
import jax.numpy as jnp
from jax import lax
from jax.experimental import pallas as pl
from jax.experimental.pallas import tpu as pltpu
from jax.sharding import PartitionSpec as P

SWEEPS = 3
CAP = 4
MESH = pl.DeviceIdType.MESH
F32 = jnp.float32
BF16 = jnp.bfloat16
FIELDS = 32


def roll(x, shift, axis):
    return pltpu.roll(x, shift % x.shape[axis], axis)


def across(a, b):
    return lax.dot_general(a, b, (((1,), (1,)), ((), ())), preferred_element_type=F32)


def kernel(
    n_gx, n_gy,
    t_h, a_h, f_h, slow_h, rows_h, tile_h, cell_h,
    adjv, gradv,
    tv, fv, a0, slv, rowsv, tilev, cellv,
    c_l, c_r, c_u, c_d, c_b, c_t, sp, total,
    rec, msg, box,
    ey_hi, ey_lo, ex, ry_hi, ry_lo, rx,
    oy_hi, oy_lo, ox, iy_lo, iy_hi, ix_lo, ix_hi,
    toy_hi, toy_lo, tox, tiy_lo, tiy_hi, tix_lo, tix_hi,
    in_sem, small_sem, send_sem, recv_sem, tsend, trecv, st_send, st_recv,
):
    sources, levels, rows_n, lanes_n = tv.shape
    devices = n_gx * n_gy
    mx = lax.axis_index("gx")
    my = lax.axis_index("gy")
    me = mx * n_gy + my

    barrier = pltpu.get_barrier_semaphore()
    others = [(dx, dy) for dx in range(n_gx) for dy in range(n_gy) if dx or dy]

    def far(dx, dy):
        return lax.rem(mx + dx, n_gx), lax.rem(my + dy, n_gy)

    for dx, dy in others:
        pl.semaphore_signal(barrier, inc=1, device_id=far(dx, dy), device_id_type=MESH)

    small = [
        pltpu.make_async_copy(src, dst, small_sem.at[k])
        for k, (src, dst) in enumerate(
            [(tile_h, tilev), (rows_h, rowsv), (cell_h, cellv), (slow_h, slv)]
        )
    ]
    for copy in small:
        copy.start()

    def load(k, src, dst, s):
        return pltpu.make_async_copy(src.at[s], dst.at[s], in_sem.at[k, s])

    for k, (src, dst) in enumerate([(t_h, tv), (a_h, a0), (f_h, fv)]):
        for s in range(sources):
            load(k, src, dst, s).start()

    sub = lax.broadcasted_iota(jnp.int32, (rows_n, lanes_n), 0)
    lane = lax.broadcasted_iota(jnp.int32, (rows_n, lanes_n), 1)
    first_row, last_row = sub == 0, sub == rows_n - 1
    first_lane, last_lane = lane == 0, lane == lanes_n - 1
    odd = lane % 2 == 1

    @pl.when(my == 0)
    def _():
        iy_lo[...] = jnp.zeros_like(iy_lo)
        tiy_lo[...] = jnp.zeros_like(tiy_lo)

    @pl.when(my == n_gy - 1)
    def _():
        iy_hi[...] = jnp.zeros_like(iy_hi)
        tiy_hi[...] = jnp.zeros_like(tiy_hi)

    @pl.when(mx == 0)
    def _():
        ix_lo[...] = jnp.zeros_like(ix_lo)
        tix_lo[...] = jnp.zeros_like(tix_lo)

    @pl.when(mx == n_gx - 1)
    def _():
        ix_hi[...] = jnp.zeros_like(ix_hi)
        tix_hi[...] = jnp.zeros_like(tix_hi)

    for copy in small[:3]:
        copy.wait()
    count = rowsv.shape[1]
    r_i = lax.broadcasted_iota(jnp.int32, (count, count), 0)
    c_i = lax.broadcasted_iota(jnp.int32, (count, count), 1)
    tile_row = tilev[...]
    cells = cellv[...]
    rec[...] = jnp.zeros_like(rec)
    rec[0:sources] = rowsv[...]
    rec[sources : sources + 1] = (cells // lanes_n).astype(F32)
    rec[sources + 1 : sources + 2] = (cells % lanes_n).astype(F32)
    d_i = lax.broadcasted_iota(jnp.int32, (devices, count), 0)
    named = jnp.where(d_i == tile_row, 1.0, 0.0)
    earlier = jnp.where(r_i < c_i, 1.0, 0.0)
    rank = jnp.dot(named.astype(BF16), earlier.astype(BF16), preferred_element_type=F32)
    base = rec[...]
    b_hi = base.astype(BF16)
    left = base - b_hi.astype(F32)
    b_mid = left.astype(BF16)
    b_lo = (left - b_mid.astype(F32)).astype(BF16)
    slots = jnp.zeros((devices, lanes_n), F32)
    for c in range(CAP):
        pick = jnp.where((named > 0.0) & (rank == float(c)), 1.0, 0.0).astype(BF16)
        got = (
            across(pick, b_lo) + across(pick, b_mid) + across(pick, b_hi)
        )
        slots = slots + (roll(got, FIELDS * c, 1) if c else got)
    for d in range(devices):
        msg[d] = slots[d : d + 1, :]

    def packed(acc, plane, z):
        return jnp.where((lane == 2 * z) | (lane == 2 * z + 1), roll(plane, 2 * z + 1, 1), acc)

    def edges_of(s, _):
        load(0, t_h, tv, s).wait()
        load(1, a_h, a0, s).wait()
        acc_t = jnp.zeros((rows_n, lanes_n), F32)
        acc_a = jnp.zeros((rows_n, lanes_n), F32)
        for z in range(levels):
            t = tv[s, z]
            a = a0[s, z]
            oy_hi[0, s, z : z + 1, :] = t[rows_n - 1 : rows_n]
            oy_lo[0, s, z : z + 1, :] = t[0:1]
            ry_hi[s, z : z + 1, :] = a[rows_n - 1 : rows_n]
            ry_lo[s, z : z + 1, :] = a[0:1]
            acc_t = packed(acc_t, t, z)
            acc_a = packed(acc_a, a, z)
        ox[0, s] = acc_t
        rx[s] = acc_a
        return 0

    lax.fori_loop(0, sources, edges_of, 0)

    pl.semaphore_wait(barrier, devices - 1)

    def halo(k, s):
        def one(way, src, dst, dev):
            return pltpu.make_async_remote_copy(
                src_ref=src.at[k, s], dst_ref=dst.at[k, s],
                send_sem=send_sem.at[k, way, s], recv_sem=recv_sem.at[k, way, s],
                device_id=dev, device_id_type=MESH,
            )
        up = (mx, lax.rem(my + 1, n_gy))
        down = (mx, lax.rem(my + n_gy - 1, n_gy))
        right = (lax.rem(mx + 1, n_gx), my)
        left_ = (lax.rem(mx + n_gx - 1, n_gx), my)
        return (
            (one(0, oy_hi, iy_lo, up), my < n_gy - 1, my > 0),
            (one(1, oy_lo, iy_hi, down), my > 0, my < n_gy - 1),
            (one(2, ox, ix_lo, right), mx < n_gx - 1, mx > 0),
            (one(3, ox, ix_hi, left_), mx > 0, mx < n_gx - 1),
        )

    def send(k, s):
        for copy, sends, _ in halo(k, s):
            @pl.when(sends)
            def _(copy=copy):
                copy.start()

    def arrive(k, s):
        for copy, _, takes in halo(k, s):
            @pl.when(takes)
            def _(copy=copy):
                copy.wait_recv()

    def send_all(s, _):
        send(0, s)
        return 0

    lax.fori_loop(0, sources, send_all, 0)

    own = pltpu.make_async_copy(msg.at[me], box.at[me], st_recv)
    for dx, dy in others:
        ox_, oy_ = far(dx, dy)
        pltpu.make_async_remote_copy(
            src_ref=msg.at[ox_ * n_gy + oy_], dst_ref=box.at[me],
            send_sem=st_send, recv_sem=st_recv,
            device_id=(ox_, oy_), device_id_type=MESH,
        ).start()
    own.start()

    def coefficients(s, _):
        load(2, f_h, fv, s).wait()
        arrive(0, s)
        acc = jnp.zeros((rows_n, lanes_n), F32)
        comb = jnp.where(odd, ix_hi[0, s], ix_lo[0, s])
        below = jnp.zeros((rows_n, lanes_n), F32)
        z_plus_before = jnp.zeros((rows_n, lanes_n), F32)
        r_before = None
        t = tv[s, 0]
        for z in range(levels):
            above = tv[s, z + 1] if z + 1 < levels else jnp.zeros((rows_n, lanes_n), F32)
            flags = fv[s, z]
            is_x, is_y, is_z = (flags & 1) == 1, (flags & 2) == 2, (flags & 4) == 4
            u = roll(comb, -(2 * z + 1), 1)
            t_l = roll(jnp.where(last_lane, u, t), 1, 1)
            t_r = roll(jnp.where(first_lane, u, t), -1, 1)
            t_u = jnp.where(first_row, iy_lo[0, s, z : z + 1, :], roll(t, 1, 0))
            t_d = jnp.where(last_row, iy_hi[0, s, z : z + 1, :], roll(t, -1, 0))
            k_x = jnp.maximum(t - jnp.where(is_x, t_r, t_l), 0.0)
            k_y = jnp.maximum(t - jnp.where(is_y, t_d, t_u), 0.0)
            k_z = jnp.maximum(t - jnp.where(is_z, above, below), 0.0)
            r = 1.0 / (1.0 + k_x + k_y + k_z)
            x_plus, x_minus = jnp.where(is_x, k_x, 0.0), jnp.where(is_x, 0.0, k_x)
            y_plus, y_minus = jnp.where(is_y, k_y, 0.0), jnp.where(is_y, 0.0, k_y)
            z_plus, z_minus = jnp.where(is_z, k_z, 0.0), jnp.where(is_z, 0.0, k_z)
            c_l[s, z] = roll(jnp.where(last_lane, 1.0, x_plus), 1, 1) * r
            c_r[s, z] = roll(jnp.where(first_lane, 1.0, x_minus), -1, 1) * r
            c_u[s, z] = roll(jnp.where(last_row, 1.0, y_plus), 1, 0) * r
            c_d[s, z] = roll(jnp.where(first_row, 1.0, y_minus), -1, 0) * r
            c_b[s, z] = z_plus_before * r
            if z:
                c_t[s, z - 1] = z_minus * r_before
            sp[s, z] = r
            ey_hi[s, z : z + 1, :] = y_plus[rows_n - 1 : rows_n]
            ey_lo[s, z : z + 1, :] = y_minus[0:1]
            acc = packed(acc, jnp.where(first_lane, x_minus, x_plus), z)
            below, t = t, above
            z_plus_before, r_before = z_plus, r
        c_t[s, levels - 1] = jnp.zeros((rows_n, lanes_n), F32)
        ex[s] = acc
        oy_hi[1, s] = ey_hi[s] * ry_hi[s]
        oy_lo[1, s] = ey_lo[s] * ry_lo[s]
        ox[1, s] = acc * rx[s]
        send(1, s)
        return 0

    lax.fori_loop(0, sources, coefficients, 0)

    pltpu.make_async_copy(box, box, st_recv).wait()
    boxes = jnp.concatenate([box[d] for d in range(devices)], axis=0)
    stacked = jnp.concatenate(
        [boxes] + [roll(boxes, -FIELDS * c, 1) for c in range(1, CAP)], axis=0
    )
    fields = stacked.T
    amount = stacked.shape[0]
    values = fields[0:sources]
    v_hi = values.astype(BF16).astype(F32)
    v_left = values - v_hi
    v_mid = v_left.astype(BF16).astype(F32)
    v_lo = v_left - v_mid
    at_row = fields[sources : sources + 1]
    at_lane = fields[sources + 1 : sources + 2]
    row_i = lax.broadcasted_iota(jnp.int32, (levels * rows_n, amount), 0).astype(F32)
    lane_i = lax.broadcasted_iota(jnp.int32, (lanes_n, amount), 0).astype(F32)
    in_row = jnp.where(row_i == at_row, 1.0, 0.0).astype(BF16)
    in_lane = lane_i == at_lane
    for s in range(sources):
        spread = None
        for part in (v_lo, v_mid, v_hi):
            weights = jnp.where(in_lane, part[s : s + 1], 0.0).astype(BF16)
            term = across(in_row, weights)
            spread = term if spread is None else spread + term
        sp[s] = sp[s] * spread.reshape(levels, rows_n, lanes_n)

    total[...] = jnp.zeros_like(total)

    def sweep(k, src, dst, s):
        last = k == SWEEPS
        arrive(k, s)
        acc = jnp.zeros((rows_n, lanes_n), F32)
        comb = jnp.where(odd, ix_hi[k, s], ix_lo[k, s])
        below = None
        a = src[s, 0]
        for z in range(levels):
            above = src[s, z + 1] if z + 1 < levels else None
            u = roll(comb, -(2 * z + 1), 1)
            a_l = roll(jnp.where(last_lane, u, a), 1, 1)
            a_r = roll(jnp.where(first_lane, u, a), -1, 1)
            a_u = jnp.where(first_row, iy_lo[k, s, z : z + 1, :], roll(a, 1, 0))
            a_d = jnp.where(last_row, iy_hi[k, s, z : z + 1, :], roll(a, -1, 0))
            out = (sp[s, z] + c_l[s, z] * a_l) + (c_r[s, z] * a_r + c_u[s, z] * a_u)
            out = out + c_d[s, z] * a_d
            if below is not None:
                out = out + c_b[s, z] * below
            if above is not None:
                out = out + c_t[s, z] * above
            dst[s, z] = out
            if last:
                total[z] = total[z] + out
            else:
                ry_hi[s, z : z + 1, :] = out[rows_n - 1 : rows_n]
                ry_lo[s, z : z + 1, :] = out[0:1]
                acc = packed(acc, out, z)
            below, a = a, above
        if not last:
            oy_hi[k + 1, s] = ey_hi[s] * ry_hi[s]
            oy_lo[k + 1, s] = ey_lo[s] * ry_lo[s]
            ox[k + 1, s] = ex[s] * acc
            send(k + 1, s)
        return 0

    held = (a0, adjv)
    for k in range(1, SWEEPS + 1):
        src, dst = held[(k - 1) % 2], held[k % 2]
        lax.fori_loop(0, sources, lambda s, _, k=k, src=src, dst=dst: sweep(k, src, dst, s), 0)

    acc = jnp.zeros((rows_n, lanes_n), F32)
    for z in range(levels):
        cells = total[z]
        toy_hi[z : z + 1, :] = cells[rows_n - 1 : rows_n]
        toy_lo[z : z + 1, :] = cells[0:1]
        acc = packed(acc, cells, z)
    tox[...] = acc

    def last_copy(way, src, dst, dev):
        return pltpu.make_async_remote_copy(
            src_ref=src, dst_ref=dst, send_sem=tsend.at[way], recv_sem=trecv.at[way],
            device_id=dev, device_id_type=MESH,
        )

    finals = (
        (last_copy(0, toy_hi, tiy_lo, (mx, lax.rem(my + 1, n_gy))), my < n_gy - 1, my > 0),
        (last_copy(1, toy_lo, tiy_hi, (mx, lax.rem(my + n_gy - 1, n_gy))), my > 0, my < n_gy - 1),
        (last_copy(2, tox, tix_lo, (lax.rem(mx + 1, n_gx), my)), mx < n_gx - 1, mx > 0),
        (last_copy(3, tox, tix_hi, (lax.rem(mx + n_gx - 1, n_gx), my)), mx > 0, mx < n_gx - 1),
    )
    for copy, sends, _ in finals:
        @pl.when(sends)
        def _(copy=copy):
            copy.start()

    def drained(s, _):
        for k in range(SWEEPS + 1):
            for copy, sends, _ in halo(k, s):
                @pl.when(sends)
                def _(copy=copy):
                    copy.wait_send()
        return 0

    lax.fori_loop(0, sources, drained, 0)
    rest = msg.at[pl.ds(0, devices - 1)]
    pltpu.make_async_copy(rest, rest, st_send).wait()
    small[3].wait()

    for copy, _, takes in finals:
        @pl.when(takes)
        def _(copy=copy):
            copy.wait_recv()

    comb = jnp.where(odd, tix_hi[...], tix_lo[...])
    for z in range(levels):
        cells = total[z]
        u = roll(comb, -(2 * z + 1), 1)
        beside = (
            roll(jnp.where(last_lane, u, cells), 1, 1)
            + roll(jnp.where(first_lane, u, cells), -1, 1)
        ) + (
            jnp.where(first_row, tiy_lo[z : z + 1, :], roll(cells, 1, 0))
            + jnp.where(last_row, tiy_hi[z : z + 1, :], roll(cells, -1, 0))
        )
        gradv[z] = slv[z] * (cells + 0.125 * (beside - 4.0 * cells))
    for copy, sends, _ in finals:
        @pl.when(sends)
        def _(copy=copy):
            copy.wait_send()


def deliver(adj_v, grad_v, adj_h, grad_h, sem):
    copies = [
        pltpu.make_async_copy(adj_v, adj_h, sem.at[0]),
        pltpu.make_async_copy(grad_v, grad_h, sem.at[1]),
    ]
    for copy in copies:
        copy.start()
    for copy in copies:
        copy.wait()


def shards(
    n_gx, n_gy,
    traveltime, adjoint_start, upwind_flags, slowness, residual_rows, station_tile, station_cell,
):
    sources, levels, rows_n, lanes_n = traveltime.shape
    devices = n_gx * n_gy
    rounds = SWEEPS + 1
    big = pltpu.VMEM(traveltime.shape, F32)
    flat = pltpu.VMEM(slowness.shape, F32)
    yrows = pltpu.VMEM((sources, levels, lanes_n), F32)
    xcols = pltpu.VMEM((sources, rows_n, lanes_n), F32)
    ymsg = pltpu.VMEM((rounds, sources, levels, lanes_n), F32)
    xmsg = pltpu.VMEM((rounds, sources, rows_n, lanes_n), F32)
    ytot = pltpu.VMEM((levels, lanes_n), F32)
    xtot = pltpu.VMEM((rows_n, lanes_n), F32)
    count = residual_rows.shape[0]
    dma = pltpu.SemaphoreType.DMA
    operands = (
        traveltime, adjoint_start, upwind_flags, slowness, residual_rows.T,
        station_tile.reshape(1, count), station_cell.reshape(1, count),
    )
    results = pl.pallas_call(
        functools.partial(kernel, n_gx, n_gy),
        out_shape=(
            jax.ShapeDtypeStruct(traveltime.shape, F32),
            jax.ShapeDtypeStruct(slowness.shape, F32),
        ),
        in_specs=[pl.BlockSpec(memory_space=pltpu.HBM)] * 7,
        out_specs=[pl.BlockSpec(memory_space=pltpu.VMEM)] * 2,
        scratch_shapes=[
            big, pltpu.VMEM(traveltime.shape, jnp.int32), big, flat,
            pltpu.VMEM((sources, count), F32),
            pltpu.VMEM((1, count), jnp.int32),
            pltpu.VMEM((1, count), jnp.int32),
            big, big, big, big, big, big, big, flat,
            pltpu.VMEM((lanes_n, count), F32),
            pltpu.VMEM((devices, 1, lanes_n), F32),
            pltpu.VMEM((devices, 1, lanes_n), F32),
            yrows, yrows, xcols, yrows, yrows, xcols,
            ymsg, ymsg, xmsg, ymsg, ymsg, xmsg, xmsg,
            ytot, ytot, xtot, ytot, ytot, xtot, xtot,
            dma((3, sources)), dma((4,)),
            dma((rounds, 4, sources)), dma((rounds, 4, sources)),
            dma((4,)), dma((4,)), dma, dma,
        ],
        compiler_params=pltpu.CompilerParams(
            collective_id=0, has_side_effects=True, vmem_limit_bytes=32 * 1024 * 1024
        ),
        name="tomography",
    )(*[pltpu.with_memory_space_constraint(v, pltpu.HBM) for v in operands])
    return pl.pallas_call(
        deliver,
        out_shape=(
            jax.ShapeDtypeStruct(traveltime.shape, F32),
            jax.ShapeDtypeStruct(slowness.shape, F32),
        ),
        in_specs=[pl.BlockSpec(memory_space=pltpu.VMEM)] * 2,
        out_specs=[pl.BlockSpec(memory_space=pltpu.HBM)] * 2,
        scratch_shapes=[dma((2,))],
        compiler_params=pltpu.CompilerParams(vmem_limit_bytes=4 * 1024 * 1024),
        name="deliver",
    )(*results)


def solution(mesh):
    wide = P(None, None, "gy", "gx")
    placed = (
        wide, wide, wide, P(None, "gy", "gx"),
        P(("gx", "gy"), None), P(("gx", "gy"), None), P(("gx", "gy")),
    )
    return jax.shard_map(
        functools.partial(shards, mesh.shape["gx"], mesh.shape["gy"]),
        mesh=mesh,
        in_specs=placed,
        out_specs=(wide, P(None, "gy", "gx")),
        check_vma=False,
    )
```

```python
import functools

import jax
import jax.numpy as jnp
from jax import lax
from jax.experimental import pallas as pl
from jax.experimental.pallas import tpu as pltpu
from jax.sharding import PartitionSpec as P

SWEEPS = 3
CAP = 4
MESH = pl.DeviceIdType.MESH
F32 = jnp.float32
BF16 = jnp.bfloat16
FIELDS = 32


def roll(x, shift, axis):
    return pltpu.roll(x, shift % x.shape[axis], axis)


def across(a, b):
    return lax.dot_general(a, b, (((1,), (1,)), ((), ())), preferred_element_type=F32)


def kernel(
    n_gx, n_gy,
    t_h, a_h, f_h, slow_h, rows_h, tile_h, cell_h,
    adjv, total, rows_lo, rows_hi, columns, slv,
    tv, fv, a0, rowsv, tilev, cellv,
    c_l, c_r, c_u, c_d, c_b, c_t, sp,
    rec, msg, box,
    ey_hi, ey_lo, ex, ry_hi, ry_lo, rx,
    oy_hi, oy_lo, ox, iy_lo, iy_hi, ix_lo, ix_hi,
    toy_hi, toy_lo, tox, tiy_lo, tiy_hi, tix_lo, tix_hi,
    in_sem, small_sem, send_sem, recv_sem, tsend, trecv, st_send, st_recv,
):
    sources, levels, rows_n, lanes_n = tv.shape
    devices = n_gx * n_gy
    mx = lax.axis_index("gx")
    my = lax.axis_index("gy")
    me = mx * n_gy + my

    barrier = pltpu.get_barrier_semaphore()
    others = [(dx, dy) for dx in range(n_gx) for dy in range(n_gy) if dx or dy]

    def far(dx, dy):
        return lax.rem(mx + dx, n_gx), lax.rem(my + dy, n_gy)

    for dx, dy in others:
        pl.semaphore_signal(barrier, inc=1, device_id=far(dx, dy), device_id_type=MESH)

    small = [
        pltpu.make_async_copy(src, dst, small_sem.at[k])
        for k, (src, dst) in enumerate(
            [(tile_h, tilev), (rows_h, rowsv), (cell_h, cellv)]
        )
    ]
    slow = pltpu.make_async_copy(slow_h, slv, small_sem.at[3])
    for copy in small:
        copy.start()

    def load(k, src, dst, s):
        return pltpu.make_async_copy(src.at[s], dst.at[s], in_sem.at[k, s])

    for k, (src, dst) in enumerate([(t_h, tv), (a_h, a0), (f_h, fv)]):
        for s in range(sources):
            load(k, src, dst, s).start()
    slow.start()

    sub = lax.broadcasted_iota(jnp.int32, (rows_n, lanes_n), 0)
    lane = lax.broadcasted_iota(jnp.int32, (rows_n, lanes_n), 1)
    first_row, last_row = sub == 0, sub == rows_n - 1
    first_lane, last_lane = lane == 0, lane == lanes_n - 1
    odd = lane % 2 == 1
    lane_pair = lane // 2

    @pl.when(my == 0)
    def _():
        iy_lo[...] = jnp.zeros_like(iy_lo)
        tiy_lo[...] = jnp.zeros_like(tiy_lo)

    @pl.when(my == n_gy - 1)
    def _():
        iy_hi[...] = jnp.zeros_like(iy_hi)
        tiy_hi[...] = jnp.zeros_like(tiy_hi)

    @pl.when(mx == 0)
    def _():
        ix_lo[...] = jnp.zeros_like(ix_lo)
        tix_lo[...] = jnp.zeros_like(tix_lo)

    @pl.when(mx == n_gx - 1)
    def _():
        ix_hi[...] = jnp.zeros_like(ix_hi)
        tix_hi[...] = jnp.zeros_like(tix_hi)

    for copy in small:
        copy.wait()
    count = rowsv.shape[1]
    r_i = lax.broadcasted_iota(jnp.int32, (count, count), 0)
    c_i = lax.broadcasted_iota(jnp.int32, (count, count), 1)
    tile_row = tilev[...]
    cells = cellv[...]
    rec[...] = jnp.zeros_like(rec)
    rec[0:sources] = rowsv[...]
    rec[sources : sources + 1] = (cells // lanes_n).astype(F32)
    rec[sources + 1 : sources + 2] = (cells % lanes_n).astype(F32)
    d_i = lax.broadcasted_iota(jnp.int32, (devices, count), 0)
    named = jnp.where(d_i == tile_row, 1.0, 0.0)
    earlier = jnp.where(r_i < c_i, 1.0, 0.0)
    rank = jnp.dot(named.astype(BF16), earlier.astype(BF16), preferred_element_type=F32)
    base = rec[...]
    b_hi = base.astype(BF16)
    left = base - b_hi.astype(F32)
    b_mid = left.astype(BF16)
    b_lo = (left - b_mid.astype(F32)).astype(BF16)
    slots = jnp.zeros((devices, lanes_n), F32)
    for c in range(CAP):
        pick = jnp.where((named > 0.0) & (rank == float(c)), 1.0, 0.0).astype(BF16)
        got = (
            across(pick, b_lo) + across(pick, b_mid) + across(pick, b_hi)
        )
        slots = slots + (roll(got, FIELDS * c, 1) if c else got)
    for d in range(devices):
        msg[d] = slots[d : d + 1, :]

    def packed(acc, plane, z):
        return jnp.where(lane_pair == z, roll(plane, 2 * z + 1, 1), acc)

    def edges_of(s, _):
        load(0, t_h, tv, s).wait()
        load(1, a_h, a0, s).wait()
        acc_t = jnp.zeros((rows_n, lanes_n), F32)
        acc_a = jnp.zeros((rows_n, lanes_n), F32)
        for z in range(levels):
            t = tv[s, z]
            a = a0[s, z]
            oy_hi[0, s, z : z + 1, :] = t[rows_n - 1 : rows_n]
            oy_lo[0, s, z : z + 1, :] = t[0:1]
            ry_hi[s, z : z + 1, :] = a[rows_n - 1 : rows_n]
            ry_lo[s, z : z + 1, :] = a[0:1]
            acc_t = packed(acc_t, t, z)
            acc_a = packed(acc_a, a, z)
        ox[0, s] = acc_t
        rx[s] = acc_a
        return 0

    lax.fori_loop(0, sources, edges_of, 0)

    pl.semaphore_wait(barrier, len(others))

    def halo(k, s):
        def one(way, src, dst, dev):
            return pltpu.make_async_remote_copy(
                src_ref=src.at[k, s], dst_ref=dst.at[k, s],
                send_sem=send_sem.at[k, way, s], recv_sem=recv_sem.at[k, way, s],
                device_id=dev, device_id_type=MESH,
            )
        up = (mx, lax.rem(my + 1, n_gy))
        down = (mx, lax.rem(my + n_gy - 1, n_gy))
        right = (lax.rem(mx + 1, n_gx), my)
        left_ = (lax.rem(mx + n_gx - 1, n_gx), my)
        return (
            (one(0, oy_hi, iy_lo, up), my < n_gy - 1, my > 0),
            (one(1, oy_lo, iy_hi, down), my > 0, my < n_gy - 1),
            (one(2, ox, ix_lo, right), mx < n_gx - 1, mx > 0),
            (one(3, ox, ix_hi, left_), mx > 0, mx < n_gx - 1),
        )

    def send(k, s):
        for copy, sends, _ in halo(k, s):
            @pl.when(sends)
            def _(copy=copy):
                copy.start()

    def arrive(k, s):
        for copy, _, takes in halo(k, s):
            @pl.when(takes)
            def _(copy=copy):
                copy.wait_recv()

    def send_all(s, _):
        send(0, s)
        return 0

    lax.fori_loop(0, sources, send_all, 0)

    pltpu.make_async_copy(msg.at[me], box.at[me], st_recv).start()
    for dx, dy in others:
        to_x, to_y = far(dx, dy)
        pltpu.make_async_remote_copy(
            src_ref=msg.at[to_x * n_gy + to_y], dst_ref=box.at[me],
            send_sem=st_send, recv_sem=st_recv,
            device_id=(to_x, to_y), device_id_type=MESH,
        ).start()

    def coefficients(s, _):
        load(2, f_h, fv, s).wait()
        arrive(0, s)
        acc = jnp.zeros((rows_n, lanes_n), F32)
        comb = jnp.where(odd, ix_hi[0, s], ix_lo[0, s])
        below = jnp.zeros((rows_n, lanes_n), F32)
        z_plus_before = jnp.zeros((rows_n, lanes_n), F32)
        r_before = None
        t = tv[s, 0]
        for z in range(levels):
            above = tv[s, z + 1] if z + 1 < levels else jnp.zeros((rows_n, lanes_n), F32)
            flags = fv[s, z]
            is_x, is_y, is_z = (flags & 1) == 1, (flags & 2) == 2, (flags & 4) == 4
            u = roll(comb, -(2 * z + 1), 1)
            t_l = roll(jnp.where(last_lane, u, t), 1, 1)
            t_r = roll(jnp.where(first_lane, u, t), -1, 1)
            t_u = jnp.where(first_row, iy_lo[0, s, z : z + 1, :], roll(t, 1, 0))
            t_d = jnp.where(last_row, iy_hi[0, s, z : z + 1, :], roll(t, -1, 0))
            k_x = jnp.maximum(t - jnp.where(is_x, t_r, t_l), 0.0)
            k_y = jnp.maximum(t - jnp.where(is_y, t_d, t_u), 0.0)
            k_z = jnp.maximum(t - jnp.where(is_z, above, below), 0.0)
            r = 1.0 / (1.0 + k_x + k_y + k_z)
            x_plus, x_minus = jnp.where(is_x, k_x, 0.0), jnp.where(is_x, 0.0, k_x)
            y_plus, y_minus = jnp.where(is_y, k_y, 0.0), jnp.where(is_y, 0.0, k_y)
            z_plus, z_minus = jnp.where(is_z, k_z, 0.0), jnp.where(is_z, 0.0, k_z)
            c_l[s, z] = roll(jnp.where(last_lane, 1.0, x_plus), 1, 1) * r
            c_r[s, z] = roll(jnp.where(first_lane, 1.0, x_minus), -1, 1) * r
            c_u[s, z] = roll(jnp.where(last_row, 1.0, y_plus), 1, 0) * r
            c_d[s, z] = roll(jnp.where(first_row, 1.0, y_minus), -1, 0) * r
            c_b[s, z] = z_plus_before * r
            if z:
                c_t[s, z - 1] = z_minus * r_before
            sp[s, z] = r
            ey_hi[s, z : z + 1, :] = y_plus[rows_n - 1 : rows_n]
            ey_lo[s, z : z + 1, :] = y_minus[0:1]
            acc = packed(acc, jnp.where(first_lane, x_minus, x_plus), z)
            below, t = t, above
            z_plus_before, r_before = z_plus, r
        c_t[s, levels - 1] = jnp.zeros((rows_n, lanes_n), F32)
        ex[s] = acc
        oy_hi[1, s] = ey_hi[s] * ry_hi[s]
        oy_lo[1, s] = ey_lo[s] * ry_lo[s]
        ox[1, s] = acc * rx[s]
        send(1, s)
        return 0

    lax.fori_loop(0, sources, coefficients, 0)

    pltpu.make_async_copy(box, box, st_recv).wait()
    boxes = jnp.concatenate([box[d] for d in range(devices)], axis=0)
    stacked = jnp.concatenate(
        [boxes] + [roll(boxes, -FIELDS * c, 1) for c in range(1, CAP)], axis=0
    )
    fields = stacked.T
    amount = stacked.shape[0]
    values = fields[0:sources]
    v_hi = values.astype(BF16).astype(F32)
    v_left = values - v_hi
    v_mid = v_left.astype(BF16).astype(F32)
    v_lo = v_left - v_mid
    at_row = fields[sources : sources + 1]
    at_lane = fields[sources + 1 : sources + 2]
    row_i = lax.broadcasted_iota(jnp.int32, (levels * rows_n, amount), 0).astype(F32)
    lane_i = lax.broadcasted_iota(jnp.int32, (lanes_n, amount), 0).astype(F32)
    in_row = jnp.where(row_i == at_row, 1.0, 0.0).astype(BF16)
    in_lane = lane_i == at_lane
    for s in range(sources):
        spread = None
        for part in (v_lo, v_mid, v_hi):
            weights = jnp.where(in_lane, part[s : s + 1], 0.0).astype(BF16)
            term = across(in_row, weights)
            spread = term if spread is None else spread + term
        sp[s] = sp[s] * spread.reshape(levels, rows_n, lanes_n)

    total[...] = jnp.zeros_like(total)

    group = 1

    def sweep(k, src, dst, first):
        last = k == SWEEPS
        members = [first * group + g for g in range(group)]
        for s in members:
            arrive(k, s)
        packs = [jnp.zeros((rows_n, lanes_n), F32)] * group
        combs = [jnp.where(odd, ix_hi[k, s], ix_lo[k, s]) for s in members]
        belows = [None] * group
        planes = [src[s, 0] for s in members]
        for z in range(levels):
            outs = []
            for g, s in enumerate(members):
                above = src[s, z + 1] if z + 1 < levels else None
                a, below = planes[g], belows[g]
                u = roll(combs[g], -(2 * z + 1), 1)
                a_l = roll(jnp.where(last_lane, u, a), 1, 1)
                a_r = roll(jnp.where(first_lane, u, a), -1, 1)
                a_u = jnp.where(first_row, iy_lo[k, s, z : z + 1, :], roll(a, 1, 0))
                a_d = jnp.where(last_row, iy_hi[k, s, z : z + 1, :], roll(a, -1, 0))
                out = (sp[s, z] + c_l[s, z] * a_l) + (c_r[s, z] * a_r + c_u[s, z] * a_u)
                out = out + c_d[s, z] * a_d
                if below is not None:
                    out = out + c_b[s, z] * below
                if above is not None:
                    out = out + c_t[s, z] * above
                dst[s, z] = out
                if not last:
                    ry_hi[s, z : z + 1, :] = out[rows_n - 1 : rows_n]
                    ry_lo[s, z : z + 1, :] = out[0:1]
                    packs[g] = packed(packs[g], out, z)
                outs.append(out)
                belows[g], planes[g] = a, above
            if last:
                total[z] = total[z] + functools.reduce(jnp.add, outs)
        if not last:
            for g, s in enumerate(members):
                oy_hi[k + 1, s] = ey_hi[s] * ry_hi[s]
                oy_lo[k + 1, s] = ey_lo[s] * ry_lo[s]
                ox[k + 1, s] = ex[s] * packs[g]
            for s in members:
                send(k + 1, s)
        return 0

    held = (a0, adjv)
    for k in range(1, SWEEPS + 1):
        src, dst = held[(k - 1) % 2], held[k % 2]
        lax.fori_loop(
            0, sources // group, lambda i, _, k=k, src=src, dst=dst: sweep(k, src, dst, i), 0
        )

    acc = jnp.zeros((rows_n, lanes_n), F32)
    for z in range(levels):
        cells = total[z]
        toy_hi[z : z + 1, :] = cells[rows_n - 1 : rows_n]
        toy_lo[z : z + 1, :] = cells[0:1]
        acc = packed(acc, cells, z)
    tox[...] = acc

    def last_copy(way, src, dst, dev):
        return pltpu.make_async_remote_copy(
            src_ref=src, dst_ref=dst, send_sem=tsend.at[way], recv_sem=trecv.at[way],
            device_id=dev, device_id_type=MESH,
        )

    finals = (
        (last_copy(0, toy_hi, tiy_lo, (mx, lax.rem(my + 1, n_gy))), my < n_gy - 1, my > 0),
        (last_copy(1, toy_lo, tiy_hi, (mx, lax.rem(my + n_gy - 1, n_gy))), my > 0, my < n_gy - 1),
        (last_copy(2, tox, tix_lo, (lax.rem(mx + 1, n_gx), my)), mx < n_gx - 1, mx > 0),
        (last_copy(3, tox, tix_hi, (lax.rem(mx + n_gx - 1, n_gx), my)), mx > 0, mx < n_gx - 1),
    )
    for copy, sends, _ in finals:
        @pl.when(sends)
        def _(copy=copy):
            copy.start()

    def drained(s, _):
        for k in range(SWEEPS + 1):
            for copy, sends, _ in halo(k, s):
                @pl.when(sends)
                def _(copy=copy):
                    copy.wait_send()
        return 0

    lax.fori_loop(0, sources, drained, 0)
    rest = msg.at[pl.ds(0, devices - 1)]
    pltpu.make_async_copy(rest, rest, st_send).wait()

    for copy, _, takes in finals:
        @pl.when(takes)
        def _(copy=copy):
            copy.wait_recv()

    slow.wait()
    rows_lo[...] = tiy_lo[...]
    rows_hi[...] = tiy_hi[...]
    columns[...] = jnp.where(odd, tix_hi[...], tix_lo[...])
    for copy, sends, _ in finals:
        @pl.when(sends)
        def _(copy=copy):
            copy.wait_send()


def deliver(adj_v, total, rows_lo, rows_hi, columns, slv, adj_h, grad_h, gradv, sem):
    whole = pltpu.make_async_copy(adj_v, adj_h, sem.at[0])
    whole.start()
    levels, rows_n, lanes_n = total.shape
    sub = lax.broadcasted_iota(jnp.int32, (rows_n, lanes_n), 0)
    lane = lax.broadcasted_iota(jnp.int32, (rows_n, lanes_n), 1)
    comb = columns[...]
    for z in range(levels):
        cells = total[z]
        u = roll(comb, -(2 * z + 1), 1)
        beside = (
            roll(jnp.where(lane == lanes_n - 1, u, cells), 1, 1)
            + roll(jnp.where(lane == 0, u, cells), -1, 1)
        ) + (
            jnp.where(sub == 0, rows_lo[z : z + 1, :], roll(cells, 1, 0))
            + jnp.where(sub == rows_n - 1, rows_hi[z : z + 1, :], roll(cells, -1, 0))
        )
        gradv[z] = slv[z] * (cells + 0.125 * (beside - 4.0 * cells))
    gradient = pltpu.make_async_copy(gradv, grad_h, sem.at[1])
    gradient.start()
    gradient.wait()
    whole.wait()


def shards(
    n_gx, n_gy,
    traveltime, adjoint_start, upwind_flags, slowness, residual_rows, station_tile, station_cell,
):
    sources, levels, rows_n, lanes_n = traveltime.shape
    devices = n_gx * n_gy
    rounds = SWEEPS + 1
    big = pltpu.VMEM(traveltime.shape, F32)
    flat = pltpu.VMEM(slowness.shape, F32)
    yrows = pltpu.VMEM((sources, levels, lanes_n), F32)
    xcols = pltpu.VMEM((sources, rows_n, lanes_n), F32)
    ymsg = pltpu.VMEM((rounds, sources, levels, lanes_n), F32)
    xmsg = pltpu.VMEM((rounds, sources, rows_n, lanes_n), F32)
    ytot = pltpu.VMEM((levels, lanes_n), F32)
    xtot = pltpu.VMEM((rows_n, lanes_n), F32)
    count = residual_rows.shape[0]
    dma = pltpu.SemaphoreType.DMA
    operands = (
        traveltime, adjoint_start, upwind_flags, slowness, residual_rows.T,
        station_tile.reshape(1, count), station_cell.reshape(1, count),
    )
    results = pl.pallas_call(
        functools.partial(kernel, n_gx, n_gy),
        out_shape=[
            jax.ShapeDtypeStruct(shape, F32)
            for shape in (
                traveltime.shape, slowness.shape, (levels, lanes_n), (levels, lanes_n),
                (rows_n, lanes_n), slowness.shape,
            )
        ],
        in_specs=[pl.BlockSpec(memory_space=pltpu.HBM)] * 7,
        out_specs=[pl.BlockSpec(memory_space=pltpu.VMEM)] * 6,
        scratch_shapes=[
            big, pltpu.VMEM(traveltime.shape, jnp.int32), big,
            pltpu.VMEM((sources, count), F32),
            pltpu.VMEM((1, count), jnp.int32),
            pltpu.VMEM((1, count), jnp.int32),
            big, big, big, big, big, big, big,
            pltpu.VMEM((lanes_n, count), F32),
            pltpu.VMEM((devices, 1, lanes_n), F32),
            pltpu.VMEM((devices, 1, lanes_n), F32),
            yrows, yrows, xcols, yrows, yrows, xcols,
            ymsg, ymsg, xmsg, ymsg, ymsg, xmsg, xmsg,
            ytot, ytot, xtot, ytot, ytot, xtot, xtot,
            dma((3, sources)), dma((4,)),
            dma((rounds, 4, sources)), dma((rounds, 4, sources)),
            dma((4,)), dma((4,)), dma, dma,
        ],
        compiler_params=pltpu.CompilerParams(
            collective_id=0, has_side_effects=True, vmem_limit_bytes=32 * 1024 * 1024
        ),
        name="tomography",
    )(*[pltpu.with_memory_space_constraint(v, pltpu.HBM) for v in operands])
    return pl.pallas_call(
        deliver,
        out_shape=(
            jax.ShapeDtypeStruct(traveltime.shape, F32),
            jax.ShapeDtypeStruct(slowness.shape, F32),
        ),
        in_specs=[pl.BlockSpec(memory_space=pltpu.VMEM)] * 6,
        out_specs=[pl.BlockSpec(memory_space=pltpu.HBM)] * 2,
        scratch_shapes=[flat, dma((2,))],
        compiler_params=pltpu.CompilerParams(vmem_limit_bytes=4 * 1024 * 1024),
        name="deliver",
    )(*results)


def solution(mesh):
    wide = P(None, None, "gy", "gx")
    placed = (
        wide, wide, wide, P(None, "gy", "gx"),
        P(("gx", "gy"), None), P(("gx", "gy"), None), P(("gx", "gy")),
    )
    return jax.shard_map(
        functools.partial(shards, mesh.shape["gx"], mesh.shape["gy"]),
        mesh=mesh,
        in_specs=placed,
        out_specs=(wide, P(None, "gy", "gx")),
        check_vma=False,
    )
```
